32 devices in a mesh: row: 4 (over y, core), col: 8 (over z, x).
Axes of the slice: x: 2, y: 2, z: 4, core: 2. Of those that a mesh axis runs over, the one named last changes fastest.
Arguments:
- adjoint_field: float32 [5, 6, 192, 3072], P(None, None, 'row', 'col'), may hold values from -6 to 6
- advect_x: float32 [6, 192, 3072], P(None, 'row', 'col'), may hold values from -0.8 to 0.8
- advect_y: float32 [6, 192, 3072], P(None, 'row', 'col'), may hold values from -0.8 to 0.8
- diffusion: float32 [5, 6, 192, 3072], P(None, None, 'row', 'col'), may hold values from 0.02 to 0.2
- zone_cells: int32 [4], replicated, may hold values from 2 to 6
- feedback_dest: int32 [8, 64, 1], P('col', 'row'), may hold values from 0 to 7; in each aligned block of 16 rows (0 to 15, 16 to 31, ..., all dimensions but the last counted through in order) at most 2 rows name the same one
- feedback_slot: int32 [8, 64, 1], P('col', 'row'), may hold values from 0 to 79
Outputs:
- nest_adjoint: float32 [5, 6, 192, 3072], P(None, None, 'row', 'col')
- parent_adjoint: float32 [5, 6, 320, 1024], P(None, None, 'row', 'col')
The draws below stay inside these ranges and needn't reach their ends.
Inputs may be any that keep to these rules, and one draw needn't show every extreme that they name: `feedback_dest`: the 16 feedback rows of one device name one destination at most 2 times, a bound that some block reaches.
All inputs are finite; a program needn't handle non-finite values.
Results may differ from the reference program's by a relative error of at most 0.00012.
Values sent between devices are 32-bit elements; how exact they have to be, the bound alone decides.
A program may use at most 192 MiB of HBM per device.

```python
import math
import jax
import jax.numpy as jnp
import numpy as np
from jax import lax

F = 5
L = 6
ITERS = 3
PROWS = 80
CXC = 16
CYC = 128
CAP = 2
NX = 192
NY = 3072
NXC = 64
NYC = 1024
NPR = 320
N_COL = 8


def plant(values, rng, low, largest):
    spot = [jax.random.randint(jax.random.fold_in(rng, axis), (), 0, length) for axis, length in enumerate(values.shape)]
    main_axis = values.shape.index(max(values.shape))
    neighbour = spot[:main_axis] + [(spot[main_axis] + 1) % values.shape[main_axis]] + spot[main_axis + 1:]
    return values.at[tuple(spot)].set(low).at[tuple(neighbour)].set(largest)


def shard_levels(key, extent, cuts, low, top_value):
    gain, own = 1.0, jax.random.fold_in(key, 6)
    for dim, blocks in cuts:
        draws = jnp.exp(jax.random.uniform(jax.random.fold_in(own, dim), (blocks,), jnp.float32, low / len(cuts), top_value / len(cuts)))
        gain = gain * jnp.repeat(draws, extent[dim] // blocks).reshape([-1 if axis == dim else 1 for axis in range(len(extent))])
    return gain


def routed_block(stream_key, own, number, rows, amount, top, bound, lean):
    order = jax.random.permutation(stream_key, amount)
    crowded, ordinary = load_shares(amount, rows * top, bound, lean, True), load_shares(amount, rows * top, bound, lean, False)
    places = jnp.arange(amount)

    def named(tallies, turn):
        used = int((tallies > 0).sum())
        fixed = max(1, used // 4)
        shifted = fixed + (places - fixed + turn * (used - fixed)) % max(1, amount - fixed)
        return jnp.zeros((amount,), jnp.int32).at[order[jnp.where(places < fixed, places, shifted)]].set(jnp.asarray(tallies, jnp.int32))

    tallies = jnp.where(number % 4 == 0, named(crowded, number // 4), named(ordinary, number - number // 4 - 1))
    mixed = jax.random.permutation(jax.random.fold_in(own, 3), amount)
    source_of, taker = mixed[0:amount // 2 * 2:2], mixed[1:amount // 2 * 2:2]
    room = jnp.minimum(tallies[source_of] - 1, bound - tallies[taker]) // 2
    room = jnp.where((source_of == order[0]) | (taker == order[0]) | (tallies[taker] == 0), 0, jnp.maximum(room, 0))
    shifted = jax.random.randint(jax.random.fold_in(own, 4), (amount // 2,), 0, 1 << 20) % (room + 1)
    tallies = tallies.at[source_of].add(-shifted).at[taker].add(shifted)
    labels = jnp.searchsorted(jnp.cumsum(tallies), jnp.arange(rows * top), side="right").astype(jnp.int32)
    table = labels.reshape(top, rows).T
    table = table[jax.random.permutation(jax.random.fold_in(own, 1), rows)]
    turn = jax.random.randint(jax.random.fold_in(own, 2), (rows, 1), 0, top)
    return jnp.take_along_axis(table, (jnp.arange(top)[None, :] + turn) % top, axis=1)


def load_shares(number_of, total, bound, skew, full):
    portions = [(1 << 20) // math.isqrt(standing ** skew) + 1 for standing in range(1, number_of + 1)]
    largest = bound if full else min(bound, max(-(-total // number_of), total * portions[0] // sum(portions)))
    least = 1 if total - largest >= number_of - 1 else 0
    counts, rest = [largest] + [least] * (number_of - 1), total - largest - least * (number_of - 1)
    while rest > 0:
        movable = [i for i in range(1, number_of) if counts[i] < largest] or [i for i in range(1, number_of) if counts[i] < bound]
        mass, budget = sum([portions[i] for i in movable]), rest
        for i in movable:
            extra = min(bound - counts[i], max(1, budget * portions[i] // mass), rest)
            counts[i] = counts[i] + extra
            rest = rest - extra
    return np.array(counts)


def centred(stream_key, extent, deviation, reach, shards=(), kind=jnp.bfloat16):
    loudness = shard_levels(stream_key, extent, shards, -0.22, 0.18) if shards else 1.0
    entries = jax.random.normal(stream_key, extent, jnp.float32) * deviation * loudness
    return jnp.minimum(jnp.maximum(entries, -reach), reach).astype(kind)


def setup_inputs(seed: int = 0) -> dict:
    streams_of = jax.random.split(jax.random.key(seed), 8)
    adjoint_field = centred(streams_of[0], (F, L, NX, NY), 1.0, 6.0, ((2, 4), (3, 8)), jnp.float32)
    advect_x = jnp.clip(jax.random.uniform(streams_of[1], (L, NX, NY), jnp.float32, -0.8, 0.8) * shard_levels(streams_of[1], (L, NX, NY), ((1, 4), (2, 8)), -0.4, 0.0), -0.8, 0.8)
    advect_y = jnp.clip(jax.random.uniform(streams_of[2], (L, NX, NY), jnp.float32, -0.8, 0.8) * shard_levels(streams_of[2], (L, NX, NY), ((1, 4), (2, 8)), -0.4, 0.0), -0.8, 0.8)
    diffusion = jnp.clip(jnp.exp(math.log(0.2) - 2.3025851 * jax.random.uniform(streams_of[3], (F, L, NX, NY), jnp.float32) ** shard_levels(streams_of[3], (F, L, NX, NY), ((2, 4), (3, 8)), -0.2, 0.2)), 0.02, 0.2)
    zone_cells = plant(jax.random.randint(streams_of[4], (4,), 2, 7), jax.random.fold_in(streams_of[4], 1), 2, 6).astype(jnp.int32)
    feedback_dest_keys = jax.random.split(jax.random.fold_in(streams_of[5], 1), N_COL * NXC // CXC)
    feedback_dest_turns = jax.random.permutation(jax.random.fold_in(streams_of[5], 3), N_COL * NXC // CXC)
    feedback_dest = jax.vmap(lambda own, number: routed_block(jax.random.fold_in(streams_of[5], 2), own, number, CXC, N_COL, 1, CAP, 2))(feedback_dest_keys, feedback_dest_turns).reshape((N_COL, NXC, 1))
    feedback_slot = plant(jax.random.randint(streams_of[6], (N_COL, NXC, 1), 0, PROWS), jax.random.fold_in(streams_of[6], 1), 0, PROWS - 1).astype(jnp.int32)
    return {"adjoint_field": adjoint_field, "advect_x": advect_x, "advect_y": advect_y, "diffusion": diffusion, "zone_cells": zone_cells, "feedback_dest": feedback_dest, "feedback_slot": feedback_slot}


def advance(widened, coef_x, coef_y, coef_d):
    flux_x = coef_x * widened
    flux_y = coef_y * widened
    spread = coef_d * widened
    center = widened[..., 1:-1, 1:-1]
    result = center + 0.5 * (flux_x[..., 2:, 1:-1] - flux_x[..., :-2, 1:-1])
    result = result + 0.5 * (flux_y[..., 1:-1, 2:] - flux_y[..., 1:-1, :-2])
    result = result + spread[..., 2:, 1:-1] + spread[..., :-2, 1:-1]
    result = result + spread[..., 1:-1, 2:] + spread[..., 1:-1, :-2]
    return result - 4.0 * spread[..., 1:-1, 1:-1]


def ramp_weight(offset, count, total, low_zone, high_zone):
    positions = offset + jnp.arange(count, dtype=jnp.int32)
    lower = jnp.maximum(low_zone - positions, 0).astype(jnp.float32) / (low_zone + 1).astype(jnp.float32)
    upper = jnp.maximum(high_zone - (total - 1 - positions), 0).astype(jnp.float32) / (high_zone + 1).astype(jnp.float32)
    return jnp.maximum(lower, upper)


def reference(adjoint_field, advect_x, advect_y, diffusion, zone_cells, feedback_dest, feedback_slot):
    cycle = ((0, 0), (1, 1), (1, 1))
    padded_x = jnp.pad(advect_x, cycle)
    padded_y = jnp.pad(advect_y, cycle)

    def per_field(pair):
        field_now, spread_coef = pair
        padded_d = jnp.pad(spread_coef, cycle)
        for sweep in range(ITERS):
            field_now = advance(jnp.pad(field_now, cycle), padded_x, padded_y, padded_d)
        return field_now

    final = lax.map(per_field, (adjoint_field, diffusion))
    weight_rows = ramp_weight(0, NX, NX, zone_cells[0], zone_cells[1])
    weight_cols = ramp_weight(0, NY, NY, zone_cells[2], zone_cells[3])
    relaxation = jnp.maximum(weight_rows[:, None], weight_cols[None, :])
    nest_adjoint = (1.0 - relaxation) * final
    weighting = (1.0 - relaxation) / 9.0 + relaxation
    coarse = (weighting * final).reshape(F, L, NXC, 3, NYC, 3).sum(axis=(3, 5))
    blocks = coarse.reshape(F, L, NXC, N_COL, CYC)
    target_rows = (jnp.arange(NXC, dtype=jnp.int32) // CXC)[:, None] * PROWS + feedback_slot[:, :, 0].T
    target_cols = feedback_dest[:, :, 0].T
    parent = jnp.zeros((F, L, NPR, N_COL, CYC), jnp.float32).at[:, :, target_rows, target_cols].add(blocks)
    return nest_adjoint, parent.reshape(F, L, NPR, NYC)
```

```python
import functools

import jax
import jax.numpy as jnp
from jax import lax
from jax.experimental import pallas as pl
from jax.experimental.pallas import tpu as pltpu
from jax.sharding import PartitionSpec as P

ITERS = 3
PROWS = 80
CAP = 2
LANES = 128
SUB = 8
PACK = 4
MESH = pl.DeviceIdType.MESH
DIRS = ((-1, 0), (1, 0), (0, 1), (0, -1), (-1, 1), (-1, -1), (1, 1), (1, -1))
NORTH, SOUTH, EAST, WEST, NE, NW, SE, SW = range(8)
OPPOSITE = (SOUTH, NORTH, WEST, EAST, SW, SE, NW, NE)


def round_up(value, step):
    return -(-value // step) * step


def split_dot(values, weights):
    high = values.astype(jnp.bfloat16)
    low = (values - high.astype(jnp.float32)).astype(jnp.bfloat16)
    return jnp.dot(high, weights, preferred_element_type=jnp.float32) + jnp.dot(
        low, weights, preferred_element_type=jnp.float32
    )


def kernel(
    dims,
    zone_ref,
    dest_ref,
    slot_ref,
    field_hbm,
    spread_hbm,
    along_x_hbm,
    along_y_hbm,
    nest_hbm,
    parent_ref,
    field,
    spread,
    along_x,
    along_y,
    nest,
    halo,
    keep,
    weigh,
    coarse,
    rows_n,
    rows_s,
    got_n,
    got_s,
    slab_e,
    slab_w,
    got_e,
    got_w,
    got_corner,
    outbound,
    arrived,
    load_sem,
    store_sem,
    send_sem,
    recv_sem,
    out_sem,
    in_sem,
):
    fields, levels, tile_rows, tiles = dims
    planes = fields * levels
    spread_at = round_up(planes, SUB)
    x_at = 2 * spread_at
    y_at = x_at + round_up(levels, SUB)
    total = y_at + round_up(levels, SUB)
    planes_pad = spread_at
    row, col = lax.axis_index("row"), lax.axis_index("col")
    nrow, ncol = lax.axis_size("row"), lax.axis_size("col")
    wide = tile_rows + SUB

    def exists(way):
        down, over = DIRS[way]
        conditions = []
        if down < 0:
            conditions.append(row > 0)
        if down > 0:
            conditions.append(row < nrow - 1)
        if over < 0:
            conditions.append(col > 0)
        if over > 0:
            conditions.append(col < ncol - 1)
        return functools.reduce(jnp.logical_and, conditions)

    def device(way):
        return (row + DIRS[way][0], col + DIRS[way][1])

    barrier = pltpu.get_barrier_semaphore()
    for way in (NORTH, SOUTH, NE, NW, SE, SW):

        @pl.when(exists(way))
        def _(way=way):
            pl.semaphore_signal(barrier, inc=1, device_id=device(way), device_id_type=MESH)

    for step in range(1, ncol):
        pl.semaphore_signal(
            barrier, inc=1, device_id=(row, lax.rem(col + step, ncol)), device_id_type=MESH
        )

    loads = []
    for kind, (source, target) in enumerate(
        ((field_hbm, field), (spread_hbm, spread), (along_x_hbm, along_x), (along_y_hbm, along_y))
    ):
        count = source.shape[0]
        for t in range(tiles):
            copy = pltpu.make_async_copy(
                source.at[:, t * LANES : (t + 1) * LANES],
                target.at[t, 0:count, :],
                load_sem.at[kind * tiles + t],
            )
            copy.start()
            loads.append(copy)

    row_index = row * tile_rows + lax.broadcasted_iota(jnp.int32, (tile_rows, LANES), 0)
    lane = lax.broadcasted_iota(jnp.int32, (tile_rows, LANES), 1)
    grid_rows, grid_cols = tile_rows * nrow, tiles * LANES * ncol

    def ramp(position, count, low_zone, high_zone):
        scale_low = jnp.full((tile_rows, LANES), (low_zone + 1).astype(jnp.float32))
        scale_high = jnp.full((tile_rows, LANES), (high_zone + 1).astype(jnp.float32))
        lower = jnp.maximum(low_zone - position, 0).astype(jnp.float32) / scale_low
        upper = jnp.maximum(high_zone - (count - 1 - position), 0).astype(jnp.float32) / scale_high
        return jnp.maximum(lower, upper)

    weight_rows = ramp(row_index, grid_rows, zone_ref[0], zone_ref[1])
    for t in range(tiles):
        weight_cols = ramp((col * tiles + t) * LANES + lane, grid_cols, zone_ref[2], zone_ref[3])
        relaxation = jnp.maximum(weight_rows, weight_cols)
        keep[t] = 1.0 - relaxation
        weigh[t] = (1.0 - relaxation) / 9.0 + relaxation
    halo[...] = jnp.zeros_like(halo)
    for t in range(tiles):
        extra = (planes_pad - planes) * tile_rows
        if extra:
            field[t, planes * tile_rows :, :] = jnp.zeros((extra, LANES), jnp.float32)

    received = {NORTH: got_n, SOUTH: got_s, EAST: got_e, WEST: got_w}
    for place, way in enumerate((NE, NW, SE, SW)):
        received[way] = got_corner.at[place]
    for way in range(8):

        @pl.when(jnp.logical_not(exists(way)))
        def _(way=way):
            received[way][...] = jnp.zeros(received[way].shape, jnp.float32)

    for copy in loads:
        copy.wait()

    for kind, pieces in enumerate(
        (((field, planes, 0),), ((spread, planes, 0),), ((along_x, levels, 0), (along_y, levels, 8)))
    ):
        first = jnp.zeros((tile_rows, LANES), jnp.float32)
        last = jnp.zeros((tile_rows, LANES), jnp.float32)
        for source, count, base in pieces:

            def pack(p, carry, source=source, base=base):
                first, last = carry
                at = pl.multiple_of(p * tile_rows, SUB)
                here = lane // PACK == p + base
                moved_first = pltpu.roll(source[0, pl.ds(at, tile_rows), :], PACK * (p + base), 1)
                moved_last = pltpu.roll(
                    source[tiles - 1, pl.ds(at, tile_rows), :], PACK * (p + base + 1), 1
                )
                return jnp.where(here, moved_first, first), jnp.where(here, moved_last, last)

            first, last = lax.fori_loop(0, count, pack, (first, last))
        slab_w[kind] = first
        slab_e[kind] = last

    for r in range(ITERS):
        for t in range(tiles):
            for source, count, base in (
                (field, planes, 0),
                (spread, planes, spread_at),
                (along_x, levels, x_at),
                (along_y, levels, y_at),
            ):
                rows_n[r * tiles + t, base : base + count, :] = source[
                    t, pl.ds(r, count, stride=tile_rows), :
                ]
                rows_s[r * tiles + t, base : base + count, :] = source[
                    t, pl.ds(tile_rows - ITERS + r, count, stride=tile_rows), :
                ]

    top, bottom = slice(0, SUB), slice(tile_rows - SUB, tile_rows)
    sources = {
        NORTH: rows_n,
        SOUTH: rows_s,
        EAST: slab_e,
        WEST: slab_w,
        NE: slab_e.at[:, top, :],
        NW: slab_w.at[:, top, :],
        SE: slab_e.at[:, bottom, :],
        SW: slab_w.at[:, bottom, :],
    }

    def remote(way):
        back = OPPOSITE[way]
        return pltpu.make_async_remote_copy(
            src_ref=sources[way],
            dst_ref=received[back],
            send_sem=send_sem.at[way],
            recv_sem=recv_sem.at[back],
            device_id=device(way),
            device_id_type=MESH,
        )

    greeted = jnp.int32(ncol - 1)
    for way in (NORTH, SOUTH, NE, NW, SE, SW):
        greeted = greeted + exists(way).astype(jnp.int32)
    pl.semaphore_wait(barrier, greeted)

    for way in range(8):

        @pl.when(exists(way))
        def _(way=way):
            remote(way).start()

    for way in range(8):

        @pl.when(exists(way))
        def _(way=way):
            pltpu.make_async_remote_copy(
                src_ref=sources[OPPOSITE[way]],
                dst_ref=received[way],
                send_sem=send_sem.at[OPPOSITE[way]],
                recv_sem=recv_sem.at[way],
                device_id=device(way),
                device_id_type=MESH,
            ).wait_recv()

    for r in range(ITERS):
        for t in range(tiles):
            halo[t, pl.ds(r, total, stride=SUB), :] = got_s[r * tiles + t]
            halo[t, pl.ds(SUB - ITERS + r, total, stride=SUB), :] = got_n[r * tiles + t]

    lane_wide = lax.broadcasted_iota(jnp.int32, (wide, LANES), 1)
    lane_low = lax.broadcasted_iota(jnp.int32, (SUB, LANES), 1)
    south_half = lax.broadcasted_iota(jnp.int32, (SUB, LANES), 0) < SUB // 2

    def block(source, p, kind, place, base):
        at = pl.multiple_of(p * tile_rows, SUB)
        low = pl.multiple_of((p + base) * SUB, SUB)
        parts = [
            jnp.concatenate([source[t, pl.ds(at, tile_rows), :], halo[t, pl.ds(low, SUB), :]], 0)
            for t in range(tiles)
        ]
        east = jnp.concatenate(
            [got_e[kind], jnp.where(south_half, got_corner[2, kind], got_corner[0, kind])], 0
        )
        west = jnp.concatenate(
            [got_w[kind], jnp.where(south_half, got_corner[3, kind], got_corner[1, kind])], 0
        )
        east = pltpu.roll(east, lax.rem(LANES - PACK * place, LANES), 1)
        west = pltpu.roll(west, LANES - PACK * (place + 1), 1)
        return parts + [jnp.where(lane_wide < LANES // 2, east, west)]

    span = tiles + 1

    def one_level(level, _):
        half_x = [0.5 * part for part in block(along_x, level, 2, level, x_at)]
        half_y = [0.5 * part for part in block(along_y, level, 2, level + 8, y_at)]

        def one_field(f, _):
            p = f * levels + level
            now = block(field, p, 0, p, 0)
            d = block(spread, p, 1, p, spread_at)
            for sweep in range(ITERS):
                done = tiles if sweep == ITERS - 1 else span
                right = [
                    pltpu.roll(now[t] * (d[t] + half_y[t]), LANES - 1, 1) for t in range(span)
                ]
                left = [pltpu.roll(now[t] * (d[t] - half_y[t]), 1, 1) for t in range(span)]
                later = []
                for t in range(done):
                    value = now[t] * (1.0 - 4.0 * d[t])
                    value = value + pltpu.roll(now[t] * (d[t] + half_x[t]), wide - 1, 0)
                    value = value + pltpu.roll(now[t] * (d[t] - half_x[t]), 1, 0)
                    value = value + jnp.where(
                        lane_wide == LANES - 1, right[(t + 1) % span], right[t]
                    )
                    value = value + jnp.where(lane_wide == 0, left[(t - 1) % span], left[t])
                    later.append(value)
                now = later
            at = pl.multiple_of(p * tile_rows, SUB)
            for t in range(tiles):
                final = now[t][:tile_rows]
                nest[t, pl.ds(at, tile_rows), :] = keep[t] * final
                field[t, pl.ds(at, tile_rows), :] = weigh[t] * final
            return 0

        return lax.fori_loop(0, fields, one_field, 0)

    lax.fori_loop(0, levels, one_level, 0)

    stores = []
    for t in range(tiles):
        copy = pltpu.make_async_copy(
            nest.at[t], nest_hbm.at[:, t * LANES : (t + 1) * LANES], store_sem.at[t]
        )
        copy.start()
        stores.append(copy)

    coarse_rows = tile_rows // 3
    gathered = []
    for t in range(tiles):
        per_row = []
        for g in range(coarse_rows):
            value = field[t, pl.ds(3 * g, planes_pad, stride=tile_rows), :]
            value = value + field[t, pl.ds(3 * g + 1, planes_pad, stride=tile_rows), :]
            value = value + field[t, pl.ds(3 * g + 2, planes_pad, stride=tile_rows), :]
            per_row.append(value)
        gathered.append(jnp.concatenate(per_row, 0))
    sums = None
    for t in range(tiles):
        fine = t * LANES + lax.broadcasted_iota(jnp.int32, (LANES, LANES), 0)
        name = lax.broadcasted_iota(jnp.int32, (LANES, LANES), 1)
        pick = (fine // 3 == name).astype(jnp.float32).astype(jnp.bfloat16)
        term = split_dot(gathered[t], pick)
        sums = term if sums is None else sums + term
    coarse[...] = sums

    dests = [dest_ref[0, g, 0] for g in range(coarse_rows)]
    spots = []
    for g in range(coarse_rows):
        rank = jnp.int32(0)
        for before in range(g):
            rank = rank + jnp.where(dests[before] == dests[g], 1, 0)
        spots.append(dests[g] * CAP + rank)
    tag_row = lax.broadcasted_iota(jnp.int32, (planes_pad, LANES), 0) == planes
    blocks = []
    for g in range(coarse_rows):
        tag = (slot_ref[0, g, 0] + 1).astype(jnp.float32)
        blocks.append(jnp.where(tag_row, tag, coarse[g * planes_pad : (g + 1) * planes_pad, :]))
    for k in range(ncol * CAP):
        value = None
        for g in range(coarse_rows):
            term = jnp.where(spots[g] == k, 1.0, 0.0) * blocks[g]
            value = term if value is None else value + term
        outbound[k // CAP, (k % CAP) * planes_pad : (k % CAP + 1) * planes_pad, :] = value

    arrived[0 : CAP * planes_pad, :] = outbound[col]

    def to_owner(step):
        owner = lax.rem(col + step, ncol)
        return pltpu.make_async_remote_copy(
            src_ref=outbound.at[owner],
            dst_ref=arrived.at[pl.ds(step * CAP * planes_pad, CAP * planes_pad), :],
            send_sem=out_sem.at[step],
            recv_sem=in_sem.at[step],
            device_id=(row, owner),
            device_id_type=MESH,
        )

    for step in range(1, ncol):
        to_owner(step).start()
    for step in range(1, ncol):
        to_owner(step).wait_recv()

    count = ncol * CAP
    tags = arrived[pl.ds(planes, count, stride=planes_pad), :]
    parent_row = lax.broadcasted_iota(jnp.int32, (count, LANES), 1).astype(jnp.float32) + 1.0
    picked = (tags == parent_row).astype(jnp.float32)
    stack = jnp.concatenate(
        [picked, picked, jnp.zeros((LANES - 2 * count, LANES), jnp.float32)], 0
    )
    picker = stack.T[:PROWS].astype(jnp.bfloat16)
    filler = jnp.zeros((LANES - 2 * count, LANES), jnp.bfloat16)
    for p in range(planes):
        value = arrived[pl.ds(p, count, stride=planes_pad), :]
        high = value.astype(jnp.bfloat16)
        low = (value - high.astype(jnp.float32)).astype(jnp.bfloat16)
        parent_ref[p] = jnp.dot(
            picker, jnp.concatenate([high, low, filler], 0), preferred_element_type=jnp.float32
        )

    for way in range(8):

        @pl.when(exists(way))
        def _(way=way):
            remote(way).wait_send()

    for step in range(1, ncol):
        to_owner(step).wait_send()
    for copy in stores:
        copy.wait()


def shards(adjoint_field, advect_x, advect_y, diffusion, zone_cells, feedback_dest, feedback_slot):
    fields, levels, tile_rows, tile_cols = adjoint_field.shape
    planes = fields * levels
    tiles = tile_cols // LANES
    nrow, ncol = lax.axis_size("row"), lax.axis_size("col")
    planes_pad = round_up(planes, SUB)
    levels_pad = round_up(levels, SUB)
    total = 2 * planes_pad + 2 * levels_pad
    own = (tiles, planes_pad * tile_rows, LANES)
    level_own = (tiles, levels * tile_rows, LANES)
    f32 = jnp.float32
    vmem = pltpu.VMEM
    dma = pltpu.SemaphoreType.DMA
    smem_spec = pl.BlockSpec(memory_space=pltpu.SMEM)
    any_spec = pl.BlockSpec(memory_space=pl.ANY)
    nest, parent = pl.pallas_call(
        functools.partial(kernel, (fields, levels, tile_rows, tiles)),
        out_shape=(
            jax.ShapeDtypeStruct((planes * tile_rows, tile_cols), f32),
            jax.ShapeDtypeStruct((planes, PROWS, LANES), f32),
        ),
        in_specs=[smem_spec] * 3 + [any_spec] * 4,
        out_specs=(any_spec, pl.BlockSpec(memory_space=pltpu.VMEM)),
        scratch_shapes=[
            vmem(own, f32),
            vmem((tiles, planes * tile_rows, LANES), f32),
            vmem(level_own, f32),
            vmem(level_own, f32),
            vmem((tiles, planes * tile_rows, LANES), f32),
            vmem((tiles, total * SUB, LANES), f32),
            vmem((tiles, tile_rows, LANES), f32),
            vmem((tiles, tile_rows, LANES), f32),
            vmem((tile_rows // 3 * planes_pad, LANES), f32),
        ]
        + [vmem((ITERS * tiles, total, LANES), f32)] * 4
        + [vmem((3, tile_rows, LANES), f32)] * 4
        + [
            vmem((4, 3, SUB, LANES), f32),
            vmem((ncol, CAP * planes_pad, LANES), f32),
            vmem((ncol * CAP * planes_pad, LANES), f32),
            dma((4 * tiles,)),
            dma((tiles,)),
            dma((8,)),
            dma((8,)),
            dma((ncol,)),
            dma((ncol,)),
        ],
        compiler_params=pltpu.CompilerParams(
            collective_id=0, has_side_effects=True, vmem_limit_bytes=60 * 1024 * 1024
        ),
    )(
        zone_cells,
        feedback_dest,
        feedback_slot,
        adjoint_field.reshape(planes * tile_rows, tile_cols),
        diffusion.reshape(planes * tile_rows, tile_cols),
        advect_x.reshape(levels * tile_rows, tile_cols),
        advect_y.reshape(levels * tile_rows, tile_cols),
    )
    return (
        nest.reshape(adjoint_field.shape),
        parent.reshape(fields, levels, PROWS, LANES),
    )


def solution(mesh):
    placed = (
        P(None, None, "row", "col"),
        P(None, "row", "col"),
        P(None, "row", "col"),
        P(None, None, "row", "col"),
        P(),
        P("col", "row", None),
        P("col", "row", None),
    )
    return jax.shard_map(
        shards,
        mesh=mesh,
        in_specs=placed,
        out_specs=(P(None, None, "row", "col"), P(None, None, "row", "col")),
        check_vma=False,
    )
```

```python
import functools

import jax
import jax.numpy as jnp
from jax import lax
from jax.experimental import pallas as pl
from jax.experimental.pallas import tpu as pltpu
from jax.sharding import PartitionSpec as P

ITERS = 3
PROWS = 80
CAP = 2
LANES = 128
SUB = 8
PACK = 4
MESH = pl.DeviceIdType.MESH
DIRS = ((-1, 0), (1, 0), (0, 1), (0, -1), (-1, 1), (-1, -1), (1, 1), (1, -1))
NORTH, SOUTH, EAST, WEST, NE, NW, SE, SW = range(8)
OPPOSITE = (SOUTH, NORTH, WEST, EAST, SW, SE, NW, NE)


def round_up(value, step):
    return -(-value // step) * step


def split_dot(values, weights):
    high = values.astype(jnp.bfloat16)
    low = (values - high.astype(jnp.float32)).astype(jnp.bfloat16)
    return jnp.dot(high, weights, preferred_element_type=jnp.float32) + jnp.dot(
        low, weights, preferred_element_type=jnp.float32
    )


def kernel(
    dims,
    zone_ref,
    dest_ref,
    slot_ref,
    field_hbm,
    spread_hbm,
    along_x_hbm,
    along_y_hbm,
    nest,
    arrived,
    field,
    spread,
    along_x,
    along_y,
    halo,
    keep,
    weigh,
    coarse,
    rows_n,
    rows_s,
    got_n,
    got_s,
    slab_e,
    slab_w,
    got_e,
    got_w,
    got_corner,
    outbound,
    load_sem,
    send_sem,
    recv_sem,
    out_sem,
    in_sem,
):
    fields, levels, tile_rows, tiles = dims
    planes = fields * levels
    spread_at = round_up(planes, SUB)
    x_at = 2 * spread_at
    y_at = x_at + round_up(levels, SUB)
    total = y_at + round_up(levels, SUB)
    planes_pad = spread_at
    row, col = lax.axis_index("row"), lax.axis_index("col")
    nrow, ncol = lax.axis_size("row"), lax.axis_size("col")
    wide = tile_rows + SUB

    def exists(way):
        down, over = DIRS[way]
        conditions = []
        if down < 0:
            conditions.append(row > 0)
        if down > 0:
            conditions.append(row < nrow - 1)
        if over < 0:
            conditions.append(col > 0)
        if over > 0:
            conditions.append(col < ncol - 1)
        return functools.reduce(jnp.logical_and, conditions)

    def device(way):
        return (row + DIRS[way][0], col + DIRS[way][1])

    barrier = pltpu.get_barrier_semaphore()
    for way in (NORTH, SOUTH, NE, NW, SE, SW):

        @pl.when(exists(way))
        def _(way=way):
            pl.semaphore_signal(barrier, inc=1, device_id=device(way), device_id_type=MESH)

    for step in range(1, ncol):
        pl.semaphore_signal(
            barrier, inc=1, device_id=(row, lax.rem(col + step, ncol)), device_id_type=MESH
        )

    loads = []
    for kind, (source, target) in enumerate(
        ((field_hbm, field), (spread_hbm, spread), (along_x_hbm, along_x), (along_y_hbm, along_y))
    ):
        count = source.shape[0]
        for t in range(tiles):
            copy = pltpu.make_async_copy(
                source.at[:, t * LANES : (t + 1) * LANES],
                target.at[t, 0:count, :],
                load_sem.at[kind * tiles + t],
            )
            copy.start()
            loads.append(copy)

    row_index = row * tile_rows + lax.broadcasted_iota(jnp.int32, (tile_rows, LANES), 0)
    lane = lax.broadcasted_iota(jnp.int32, (tile_rows, LANES), 1)
    grid_rows, grid_cols = tile_rows * nrow, tiles * LANES * ncol

    def ramp(position, count, low_zone, high_zone):
        scale_low = jnp.full((tile_rows, LANES), (low_zone + 1).astype(jnp.float32))
        scale_high = jnp.full((tile_rows, LANES), (high_zone + 1).astype(jnp.float32))
        lower = jnp.maximum(low_zone - position, 0).astype(jnp.float32) / scale_low
        upper = jnp.maximum(high_zone - (count - 1 - position), 0).astype(jnp.float32) / scale_high
        return jnp.maximum(lower, upper)

    weight_rows = ramp(row_index, grid_rows, zone_ref[0], zone_ref[1])
    for t in range(tiles):
        weight_cols = ramp((col * tiles + t) * LANES + lane, grid_cols, zone_ref[2], zone_ref[3])
        relaxation = jnp.maximum(weight_rows, weight_cols)
        keep[t] = 1.0 - relaxation
        weigh[t] = (1.0 - relaxation) / 9.0 + relaxation
    halo[...] = jnp.zeros_like(halo)
    for t in range(tiles):
        extra = (planes_pad - planes) * tile_rows
        if extra:
            field[t, planes * tile_rows :, :] = jnp.zeros((extra, LANES), jnp.float32)

    received = {NORTH: got_n, SOUTH: got_s, EAST: got_e, WEST: got_w}
    for place, way in enumerate((NE, NW, SE, SW)):
        received[way] = got_corner.at[place]
    for way in range(8):

        @pl.when(jnp.logical_not(exists(way)))
        def _(way=way):
            received[way][...] = jnp.zeros(received[way].shape, jnp.float32)

    for copy in loads:
        copy.wait()

    for kind, pieces in enumerate(
        (((field, planes, 0),), ((spread, planes, 0),), ((along_x, levels, 0), (along_y, levels, 8)))
    ):
        first = jnp.zeros((tile_rows, LANES), jnp.float32)
        last = jnp.zeros((tile_rows, LANES), jnp.float32)
        for source, count, base in pieces:

            def pack(p, carry, source=source, base=base):
                first, last = carry
                at = pl.multiple_of(p * tile_rows, SUB)
                here = lane // PACK == p + base
                moved_first = pltpu.roll(source[0, pl.ds(at, tile_rows), :], PACK * (p + base), 1)
                moved_last = pltpu.roll(
                    source[tiles - 1, pl.ds(at, tile_rows), :], PACK * (p + base + 1), 1
                )
                return jnp.where(here, moved_first, first), jnp.where(here, moved_last, last)

            first, last = lax.fori_loop(0, count, pack, (first, last), unroll=6)
        slab_w[kind] = first
        slab_e[kind] = last

    for r in range(ITERS):
        for t in range(tiles):
            for source, count, base in (
                (field, planes, 0),
                (spread, planes, spread_at),
                (along_x, levels, x_at),
                (along_y, levels, y_at),
            ):
                rows_n[r * tiles + t, base : base + count, :] = source[
                    t, pl.ds(r, count, stride=tile_rows), :
                ]
                rows_s[r * tiles + t, base : base + count, :] = source[
                    t, pl.ds(tile_rows - ITERS + r, count, stride=tile_rows), :
                ]

    top, bottom = slice(0, SUB), slice(tile_rows - SUB, tile_rows)
    sources = {
        NORTH: rows_n,
        SOUTH: rows_s,
        EAST: slab_e,
        WEST: slab_w,
        NE: slab_e.at[:, top, :],
        NW: slab_w.at[:, top, :],
        SE: slab_e.at[:, bottom, :],
        SW: slab_w.at[:, bottom, :],
    }

    def remote(way):
        back = OPPOSITE[way]
        return pltpu.make_async_remote_copy(
            src_ref=sources[way],
            dst_ref=received[back],
            send_sem=send_sem.at[way],
            recv_sem=recv_sem.at[back],
            device_id=device(way),
            device_id_type=MESH,
        )

    greeted = jnp.int32(ncol - 1)
    for way in (NORTH, SOUTH, NE, NW, SE, SW):
        greeted = greeted + exists(way).astype(jnp.int32)
    pl.semaphore_wait(barrier, greeted)

    for way in range(8):

        @pl.when(exists(way))
        def _(way=way):
            remote(way).start()

    for way in range(8):

        @pl.when(exists(way))
        def _(way=way):
            pltpu.make_async_remote_copy(
                src_ref=sources[OPPOSITE[way]],
                dst_ref=received[way],
                send_sem=send_sem.at[OPPOSITE[way]],
                recv_sem=recv_sem.at[way],
                device_id=device(way),
                device_id_type=MESH,
            ).wait_recv()

    for r in range(ITERS):
        for t in range(tiles):
            halo[t, pl.ds(r, total, stride=SUB), :] = got_s[r * tiles + t]
            halo[t, pl.ds(SUB - ITERS + r, total, stride=SUB), :] = got_n[r * tiles + t]

    lane_wide = lax.broadcasted_iota(jnp.int32, (wide, LANES), 1)
    lane_low = lax.broadcasted_iota(jnp.int32, (SUB, LANES), 1)
    south_half = lax.broadcasted_iota(jnp.int32, (SUB, LANES), 0) < SUB // 2

    def block(source, p, kind, place, base):
        at = pl.multiple_of(p * tile_rows, SUB)
        low = pl.multiple_of((p + base) * SUB, SUB)
        parts = [
            jnp.concatenate([source[t, pl.ds(at, tile_rows), :], halo[t, pl.ds(low, SUB), :]], 0)
            for t in range(tiles)
        ]
        east = jnp.concatenate(
            [got_e[kind], jnp.where(south_half, got_corner[2, kind], got_corner[0, kind])], 0
        )
        west = jnp.concatenate(
            [got_w[kind], jnp.where(south_half, got_corner[3, kind], got_corner[1, kind])], 0
        )
        east = pltpu.roll(east, lax.rem(LANES - PACK * place, LANES), 1)
        west = pltpu.roll(west, LANES - PACK * (place + 1), 1)
        return parts + [jnp.where(lane_wide < LANES // 2, east, west)]

    span = tiles + 1

    def one_level(level, _):
        half_x = [0.5 * part for part in block(along_x, level, 2, level, x_at)]
        half_y = [0.5 * part for part in block(along_y, level, 2, level + 8, y_at)]

        def one_field(f, _):
            p = f * levels + level
            now = block(field, p, 0, p, 0)
            d = block(spread, p, 1, p, spread_at)
            for sweep in range(ITERS):
                done = tiles if sweep == ITERS - 1 else span
                right = [
                    pltpu.roll(now[t] * (d[t] + half_y[t]), LANES - 1, 1) for t in range(span)
                ]
                left = [pltpu.roll(now[t] * (d[t] - half_y[t]), 1, 1) for t in range(span)]
                later = []
                for t in range(done):
                    value = now[t] * (1.0 - 4.0 * d[t])
                    value = value + pltpu.roll(now[t] * (d[t] + half_x[t]), wide - 1, 0)
                    value = value + pltpu.roll(now[t] * (d[t] - half_x[t]), 1, 0)
                    value = value + jnp.where(
                        lane_wide == LANES - 1, right[(t + 1) % span], right[t]
                    )
                    value = value + jnp.where(lane_wide == 0, left[(t - 1) % span], left[t])
                    later.append(value)
                now = later
            at = pl.multiple_of(p * tile_rows, SUB)
            for t in range(tiles):
                final = now[t][:tile_rows]
                nest[t, pl.ds(at, tile_rows), :] = keep[t] * final
                field[t, pl.ds(at, tile_rows), :] = weigh[t] * final
            return 0

        return lax.fori_loop(0, fields, one_field, 0)

    lax.fori_loop(0, levels, one_level, 0)

    coarse_rows = tile_rows // 3
    gathered = []
    for t in range(tiles):
        per_row = []
        for g in range(coarse_rows):
            value = field[t, pl.ds(3 * g, planes_pad, stride=tile_rows), :]
            value = value + field[t, pl.ds(3 * g + 1, planes_pad, stride=tile_rows), :]
            value = value + field[t, pl.ds(3 * g + 2, planes_pad, stride=tile_rows), :]
            per_row.append(value)
        gathered.append(jnp.concatenate(per_row, 0))
    sums = None
    for t in range(tiles):
        fine = t * LANES + lax.broadcasted_iota(jnp.int32, (LANES, LANES), 0)
        name = lax.broadcasted_iota(jnp.int32, (LANES, LANES), 1)
        pick = (fine // 3 == name).astype(jnp.float32).astype(jnp.bfloat16)
        term = split_dot(gathered[t], pick)
        sums = term if sums is None else sums + term
    coarse[...] = sums

    dests = [dest_ref[g] for g in range(coarse_rows)]
    spots = []
    for g in range(coarse_rows):
        rank = jnp.int32(0)
        for before in range(g):
            rank = rank + jnp.where(dests[before] == dests[g], 1, 0)
        spots.append(dests[g] * CAP + rank)
    tag_row = lax.broadcasted_iota(jnp.int32, (planes_pad, LANES), 0) == planes
    blocks = []
    for g in range(coarse_rows):
        tag = (slot_ref[g] + 1).astype(jnp.float32)
        blocks.append(jnp.where(tag_row, tag, coarse[g * planes_pad : (g + 1) * planes_pad, :]))
    for k in range(ncol * CAP):
        value = None
        for g in range(coarse_rows):
            term = jnp.where(spots[g] == k, 1.0, 0.0) * blocks[g]
            value = term if value is None else value + term
        outbound[k // CAP, (k % CAP) * planes_pad : (k % CAP + 1) * planes_pad, :] = value

    arrived[0 : CAP * planes_pad, :] = outbound[col]

    def to_owner(step):
        owner = lax.rem(col + step, ncol)
        return pltpu.make_async_remote_copy(
            src_ref=outbound.at[owner],
            dst_ref=arrived.at[pl.ds(step * CAP * planes_pad, CAP * planes_pad), :],
            send_sem=out_sem.at[step],
            recv_sem=in_sem.at[step],
            device_id=(row, owner),
            device_id_type=MESH,
        )

    for step in range(1, ncol):
        to_owner(step).start()
    for step in range(1, ncol):
        to_owner(step).wait_recv()

    for way in range(8):

        @pl.when(exists(way))
        def _(way=way):
            remote(way).wait_send()

    for step in range(1, ncol):
        to_owner(step).wait_send()


def finish(dims, nest, arrived, nest_hbm, parent_ref, store_sem):
    planes, tiles, ncol = dims
    planes_pad = round_up(planes, SUB)
    stores = []
    for t in range(tiles):
        copy = pltpu.make_async_copy(
            nest.at[t], nest_hbm.at[:, t * LANES : (t + 1) * LANES], store_sem.at[t]
        )
        copy.start()
        stores.append(copy)

    count = ncol * CAP
    tags = arrived[pl.ds(planes, count, stride=planes_pad), :]
    parent_row = lax.broadcasted_iota(jnp.int32, (count, LANES), 1).astype(jnp.float32) + 1.0
    picked = (tags == parent_row).astype(jnp.float32)
    stack = jnp.concatenate(
        [picked, picked, jnp.zeros((LANES - 2 * count, LANES), jnp.float32)], 0
    )
    picker = stack.T[:PROWS].astype(jnp.bfloat16)
    filler = jnp.zeros((LANES - 2 * count, LANES), jnp.bfloat16)
    for p in range(planes):
        value = arrived[pl.ds(p, count, stride=planes_pad), :]
        high = value.astype(jnp.bfloat16)
        low = (value - high.astype(jnp.float32)).astype(jnp.bfloat16)
        parent_ref[p] = jnp.dot(
            picker, jnp.concatenate([high, low, filler], 0), preferred_element_type=jnp.float32
        )

    for copy in stores:
        copy.wait()


def shards(adjoint_field, advect_x, advect_y, diffusion, zone_cells, feedback_dest, feedback_slot):
    fields, levels, tile_rows, tile_cols = adjoint_field.shape
    planes = fields * levels
    tiles = tile_cols // LANES
    nrow, ncol = lax.axis_size("row"), lax.axis_size("col")
    planes_pad = round_up(planes, SUB)
    levels_pad = round_up(levels, SUB)
    total = 2 * planes_pad + 2 * levels_pad
    own = (tiles, planes_pad * tile_rows, LANES)
    level_own = (tiles, levels * tile_rows, LANES)
    f32 = jnp.float32
    vmem = pltpu.VMEM
    dma = pltpu.SemaphoreType.DMA
    smem_spec = pl.BlockSpec(memory_space=pltpu.SMEM)
    any_spec = pl.BlockSpec(memory_space=pl.ANY)
    nest_shape = (tiles, planes * tile_rows, LANES)
    arrived_shape = (ncol * CAP * planes_pad, LANES)
    vmem_spec = pl.BlockSpec(memory_space=pltpu.VMEM)
    nest, arrived = pl.pallas_call(
        functools.partial(kernel, (fields, levels, tile_rows, tiles)),
        out_shape=(pltpu.VMEM(nest_shape, f32), pltpu.VMEM(arrived_shape, f32)),
        in_specs=[smem_spec] * 3 + [any_spec] * 4,
        out_specs=(vmem_spec, vmem_spec),
        scratch_shapes=[
            vmem(own, f32),
            vmem((tiles, planes * tile_rows, LANES), f32),
            vmem(level_own, f32),
            vmem(level_own, f32),
            vmem((tiles, total * SUB, LANES), f32),
            vmem((tiles, tile_rows, LANES), f32),
            vmem((tiles, tile_rows, LANES), f32),
            vmem((tile_rows // 3 * planes_pad, LANES), f32),
        ]
        + [vmem((ITERS * tiles, total, LANES), f32)] * 4
        + [vmem((3, tile_rows, LANES), f32)] * 4
        + [
            vmem((4, 3, SUB, LANES), f32),
            vmem((ncol, CAP * planes_pad, LANES), f32),
            dma((4 * tiles,)),
            dma((8,)),
            dma((8,)),
            dma((ncol,)),
            dma((ncol,)),
        ],
        compiler_params=pltpu.CompilerParams(
            collective_id=0, has_side_effects=True, vmem_limit_bytes=61 * 1024 * 1024
        ),
    )(
        zone_cells,
        feedback_dest.reshape(-1),
        feedback_slot.reshape(-1),
        adjoint_field.reshape(planes * tile_rows, tile_cols),
        diffusion.reshape(planes * tile_rows, tile_cols),
        advect_x.reshape(levels * tile_rows, tile_cols),
        advect_y.reshape(levels * tile_rows, tile_cols),
    )
    nest, parent = pl.pallas_call(
        functools.partial(finish, (planes, tiles, ncol)),
        out_shape=(
            jax.ShapeDtypeStruct((planes * tile_rows, tile_cols), f32),
            jax.ShapeDtypeStruct((planes, PROWS, LANES), f32),
        ),
        in_specs=[vmem_spec, vmem_spec],
        out_specs=(any_spec, vmem_spec),
        scratch_shapes=[dma((tiles,))],
        compiler_params=pltpu.CompilerParams(vmem_limit_bytes=16 * 1024 * 1024),
    )(nest, arrived)
    return (
        nest.reshape(adjoint_field.shape),
        parent.reshape(fields, levels, PROWS, LANES),
    )


def solution(mesh):
    placed = (
        P(None, None, "row", "col"),
        P(None, "row", "col"),
        P(None, "row", "col"),
        P(None, None, "row", "col"),
        P(),
        P("col", "row", None),
        P("col", "row", None),
    )
    return jax.shard_map(
        shards,
        mesh=mesh,
        in_specs=placed,
        out_specs=(P(None, None, "row", "col"), P(None, None, "row", "col")),
        check_vma=False,
    )
```

```python
import functools

import jax
import jax.numpy as jnp
from jax import lax
from jax.experimental import pallas as pl
from jax.experimental.pallas import tpu as pltpu
from jax.sharding import PartitionSpec as P

ITERS = 3
PROWS = 80
CAP = 2
LANES = 128
SUB = 8
PACK = 4
MESH = pl.DeviceIdType.MESH
DIRS = ((-1, 0), (1, 0), (0, 1), (0, -1), (-1, 1), (-1, -1), (1, 1), (1, -1))
NORTH, SOUTH, EAST, WEST, NE, NW, SE, SW = range(8)
OPPOSITE = (SOUTH, NORTH, WEST, EAST, SW, SE, NW, NE)


def round_up(value, step):
    return -(-value // step) * step


def level_groups(fields, levels):
    groups, start = [], 0
    while start < levels:
        stop = start + -(-(levels - start) // 2)
        groups.append((start, stop, round_up((stop - start) * fields + 1, SUB)))
        start = stop
    return groups


def split_dot(values, weights):
    high = values.astype(jnp.bfloat16)
    low = (values - high.astype(jnp.float32)).astype(jnp.bfloat16)
    return jnp.dot(high, weights, preferred_element_type=jnp.float32) + jnp.dot(
        low, weights, preferred_element_type=jnp.float32
    )


def kernel(
    dims,
    zone_ref,
    dest_ref,
    slot_ref,
    field_hbm,
    spread_hbm,
    along_x_hbm,
    along_y_hbm,
    *refs,
):
    count_groups = len(level_groups(dims[0], dims[1]))
    nest, arrived = refs[0], refs[1 : 1 + count_groups]
    outbound = refs[1 + count_groups : 1 + 2 * count_groups]
    (
    field,
    spread,
    along_x,
    along_y,
    halo,
    keep,
    weigh,
    coarse,
    rows_n,
    rows_s,
    got_n,
    got_s,
    slab_e,
    slab_w,
    got_e,
    got_w,
    got_corner,
    got_own,
    edges,
    weighted,
    load_sem,
    send_sem,
    recv_sem,
    out_sem,
    in_sem,
    ) = refs[1 + 2 * count_groups :]
    fields, levels, tile_rows, tiles = dims
    planes = fields * levels
    spread_at = round_up(planes, SUB)
    x_at = 2 * spread_at
    y_at = x_at + round_up(levels, SUB)
    total = y_at + round_up(levels, SUB)
    planes_pad = spread_at
    row, col = lax.axis_index("row"), lax.axis_index("col")
    nrow, ncol = lax.axis_size("row"), lax.axis_size("col")
    wide = tile_rows + SUB

    def exists(way):
        down, over = DIRS[way]
        conditions = []
        if down < 0:
            conditions.append(row > 0)
        if down > 0:
            conditions.append(row < nrow - 1)
        if over < 0:
            conditions.append(col > 0)
        if over > 0:
            conditions.append(col < ncol - 1)
        return functools.reduce(jnp.logical_and, conditions)

    def device(way):
        return (row + DIRS[way][0], col + DIRS[way][1])

    barrier = pltpu.get_barrier_semaphore()
    for way in (NORTH, SOUTH, NE, NW, SE, SW):

        @pl.when(exists(way))
        def _(way=way):
            pl.semaphore_signal(barrier, inc=1, device_id=device(way), device_id_type=MESH)

    for step in range(1, ncol):
        pl.semaphore_signal(
            barrier, inc=1, device_id=(row, lax.rem(col + step, ncol)), device_id_type=MESH
        )

    loads = []
    for kind, (source, target) in enumerate(
        ((field_hbm, field), (spread_hbm, spread), (along_x_hbm, along_x), (along_y_hbm, along_y))
    ):
        count = source.shape[0]
        for t in range(tiles):
            copy = pltpu.make_async_copy(
                source.at[:, t * LANES : (t + 1) * LANES],
                target.at[t, 0:count, :],
                load_sem.at[kind * tiles + t],
            )
            copy.start()
            loads.append(copy)

    row_index = row * tile_rows + lax.broadcasted_iota(jnp.int32, (tile_rows, LANES), 0)
    lane = lax.broadcasted_iota(jnp.int32, (tile_rows, LANES), 1)
    grid_rows, grid_cols = tile_rows * nrow, tiles * LANES * ncol

    def ramp(position, count, low_zone, high_zone):
        scale_low = jnp.full((tile_rows, LANES), (low_zone + 1).astype(jnp.float32))
        scale_high = jnp.full((tile_rows, LANES), (high_zone + 1).astype(jnp.float32))
        lower = jnp.maximum(low_zone - position, 0).astype(jnp.float32) / scale_low
        upper = jnp.maximum(high_zone - (count - 1 - position), 0).astype(jnp.float32) / scale_high
        return jnp.maximum(lower, upper)

    weight_rows = ramp(row_index, grid_rows, zone_ref[0], zone_ref[1])
    for t in range(tiles):
        weight_cols = ramp((col * tiles + t) * LANES + lane, grid_cols, zone_ref[2], zone_ref[3])
        relaxation = jnp.maximum(weight_rows, weight_cols)
        keep[t] = 1.0 - relaxation
        weigh[t] = (1.0 - relaxation) / 9.0 + relaxation
    halo[...] = jnp.zeros_like(halo)
    received = {NORTH: got_n, SOUTH: got_s, EAST: got_e, WEST: got_w}
    for place, way in enumerate((NE, NW, SE, SW)):
        received[way] = got_corner.at[place]
    for way in range(8):

        @pl.when(jnp.logical_not(exists(way)))
        def _(way=way):
            received[way][...] = jnp.zeros(received[way].shape, jnp.float32)
            if way in (NORTH, SOUTH):
                for side in range(2):
                    shape = got_own.shape[1:]
                    got_own[2 * side + way] = jnp.zeros(shape, jnp.float32)

    for copy in loads:
        copy.wait()

    for kind, pieces in enumerate(
        (((field, planes, 0),), ((spread, planes, 0),), ((along_x, levels, 0), (along_y, levels, 8)))
    ):
        first = jnp.zeros((tile_rows, LANES), jnp.float32)
        last = jnp.zeros((tile_rows, LANES), jnp.float32)
        for source, count, base in pieces:

            def pack(p, carry, source=source, base=base):
                first, last = carry
                at = pl.multiple_of(p * tile_rows, SUB)
                here = lane // PACK == p + base
                moved_first = pltpu.roll(source[0, pl.ds(at, tile_rows), :], PACK * (p + base), 1)
                moved_last = pltpu.roll(
                    source[tiles - 1, pl.ds(at, tile_rows), :], PACK * (p + base + 1), 1
                )
                return jnp.where(here, moved_first, first), jnp.where(here, moved_last, last)

            first, last = lax.fori_loop(0, count, pack, (first, last), unroll=6)
        slab_w[kind] = first
        slab_e[kind] = last

    for r in range(ITERS):
        for t in range(tiles):
            for source, count, base in (
                (field, planes, 0),
                (spread, planes, spread_at),
                (along_x, levels, x_at),
                (along_y, levels, y_at),
            ):
                rows_n[r * tiles + t, base : base + count, :] = source[
                    t, pl.ds(r, count, stride=tile_rows), :
                ]
                rows_s[r * tiles + t, base : base + count, :] = source[
                    t, pl.ds(tile_rows - ITERS + r, count, stride=tile_rows), :
                ]

    top, bottom = slice(0, SUB), slice(tile_rows - SUB, tile_rows)
    sources = {
        NORTH: rows_n,
        SOUTH: rows_s,
        EAST: slab_e,
        WEST: slab_w,
        NE: slab_e.at[:, top, :],
        NW: slab_w.at[:, top, :],
        SE: slab_e.at[:, bottom, :],
        SW: slab_w.at[:, bottom, :],
    }

    def remote(way):
        back = OPPOSITE[way]
        return pltpu.make_async_remote_copy(
            src_ref=sources[way],
            dst_ref=received[back],
            send_sem=send_sem.at[way],
            recv_sem=recv_sem.at[back],
            device_id=device(way),
            device_id_type=MESH,
        )

    def own_columns(way, side, arriving):
        back = OPPOSITE[way]
        sent = back if arriving else way
        place = 2 * side + (way if arriving else back)
        slab = (slab_e, slab_w)[side]
        return pltpu.make_async_remote_copy(
            src_ref=slab.at[:, top if sent == NORTH else bottom, :],
            dst_ref=got_own.at[place],
            send_sem=send_sem.at[8 + 2 * side + sent],
            recv_sem=recv_sem.at[8 + place],
            device_id=device(way),
            device_id_type=MESH,
        )

    greeted = jnp.int32(ncol - 1)
    for way in (NORTH, SOUTH, NE, NW, SE, SW):
        greeted = greeted + exists(way).astype(jnp.int32)
    pl.semaphore_wait(barrier, greeted)

    for way in range(8):

        @pl.when(exists(way))
        def _(way=way):
            if way in (NORTH, SOUTH):
                for side in range(2):
                    own_columns(way, side, False).start()
            remote(way).start()

    for way in range(8):

        @pl.when(exists(way))
        def _(way=way):
            pltpu.make_async_remote_copy(
                src_ref=sources[OPPOSITE[way]],
                dst_ref=received[way],
                send_sem=send_sem.at[OPPOSITE[way]],
                recv_sem=recv_sem.at[way],
                device_id=device(way),
                device_id_type=MESH,
            ).wait_recv()
            if way in (NORTH, SOUTH):
                for side in range(2):
                    own_columns(way, side, True).wait_recv()

    for r in range(ITERS):
        for t in range(tiles):
            halo[t, pl.ds(r, total, stride=SUB), :] = got_s[r * tiles + t]
            halo[t, pl.ds(SUB - ITERS + r, total, stride=SUB), :] = got_n[r * tiles + t]

    lane_wide = lax.broadcasted_iota(jnp.int32, (wide, LANES), 1)
    lane_low = lax.broadcasted_iota(jnp.int32, (SUB, LANES), 1)
    south_half = lax.broadcasted_iota(jnp.int32, (SUB, LANES), 0) < SUB // 2

    def block(source, p, base):
        at = pl.multiple_of(p * tile_rows, SUB)
        low = pl.multiple_of((p + base) * SUB, SUB)
        return [
            jnp.concatenate([source[t, pl.ds(at, tile_rows), :], halo[t, pl.ds(low, SUB), :]], 0)
            for t in range(tiles)
        ]

    def advance(now, d, half_x, half_y, rights, lefts, count):
        later = []
        for t in range(count):
            value = now[t] * (1.0 - 4.0 * d[t])
            value = value + pltpu.roll(now[t] * (d[t] + half_x[t]), wide - 1, 0)
            value = value + pltpu.roll(now[t] * (d[t] - half_x[t]), 1, 0)
            later.append(value + rights[t] + lefts[t])
        return later

    def with_rows(slab, kind, from_south, from_north):
        return jnp.concatenate([slab[kind], jnp.where(south_half, from_south, from_north)], 0)

    period = PACK * levels

    def each_field(slab, base):
        value = None
        for f in range(fields):
            moved = pltpu.roll(slab, (period * f - PACK * base) % LANES, 1)
            value = moved if value is None else jnp.where(lane_wide >= period * f, moved, value)
        return value

    inner = lane_wide % PACK
    for side in range(2):
        own, other = ((slab_e, got_e), (slab_w, got_w))[side]
        below, above = ((2, 0), (3, 1))[side]
        kinds = []
        for kind in range(3):
            pair = [
                with_rows(own, kind, got_own[2 * side + SOUTH, kind], got_own[2 * side + NORTH, kind]),
                with_rows(other, kind, got_corner[below, kind], got_corner[above, kind]),
            ]
            kinds.append(pair if side == 0 else pair[::-1])
        now, d, along = kinds
        half_x = [0.5 * each_field(part, 0) for part in along]
        half_y = [0.5 * each_field(part, 8) for part in along]
        for sweep in range(ITERS):
            right = [now[t] * (d[t] + half_y[t]) for t in range(2)]
            left = [now[t] * (d[t] - half_y[t]) for t in range(2)]
            edges[side, sweep] = right[1] if side == 0 else left[0]
            if sweep < ITERS - 1:
                rights = [
                    jnp.where(
                        inner == PACK - 1,
                        pltpu.roll(right[1], PACK - 1, 1),
                        pltpu.roll(right[0], LANES - 1, 1),
                    ),
                    pltpu.roll(right[1], LANES - 1, 1),
                ]
                lefts = [
                    pltpu.roll(left[0], 1, 1),
                    jnp.where(
                        inner == 0,
                        pltpu.roll(left[0], LANES - PACK + 1, 1),
                        pltpu.roll(left[1], 1, 1),
                    ),
                ]
                now = advance(now, d, half_x, half_y, rights, lefts, 2)

    def one_level(level, _):
        half_x = [0.5 * part for part in block(along_x, level, x_at)]
        half_y = [0.5 * part for part in block(along_y, level, y_at)]

        def one_field(f, _):
            p = f * levels + level
            now = block(field, p, 0)
            d = block(spread, p, spread_at)
            for sweep in range(ITERS):
                right = [
                    pltpu.roll(now[t] * (d[t] + half_y[t]), LANES - 1, 1) for t in range(tiles)
                ]
                left = [pltpu.roll(now[t] * (d[t] - half_y[t]), 1, 1) for t in range(tiles)]
                right.append(pltpu.roll(edges[0, sweep], LANES - 1 - PACK * p, 1))
                left.append(pltpu.roll(edges[1, sweep], LANES - PACK + 1 - PACK * p, 1))
                rights = [
                    jnp.where(lane_wide == LANES - 1, right[t + 1], right[t]) for t in range(tiles)
                ]
                lefts = [jnp.where(lane_wide == 0, left[t - 1], left[t]) for t in range(tiles)]
                now = advance(now, d, half_x, half_y, rights, lefts, tiles)
            at = pl.multiple_of(p * tile_rows, SUB)
            to = pl.multiple_of((level * fields + f) * tile_rows, SUB)
            for t in range(tiles):
                final = now[t][:tile_rows]
                nest[t, pl.ds(at, tile_rows), :] = keep[t] * final
                weighted[t, pl.ds(to, tile_rows), :] = weigh[t] * final
            return 0

        return lax.fori_loop(0, fields, one_field, 0)

    coarse_rows = tile_rows // 3
    dests = [dest_ref[g] for g in range(coarse_rows)]
    spots = []
    for g in range(coarse_rows):
        rank = jnp.int32(0)
        for before in range(g):
            rank = rank + jnp.where(dests[before] == dests[g], 1, 0)
        spots.append(dests[g] * CAP + rank)

    def to_owner(group, step):
        owner = lax.rem(col + step, ncol)
        rows = CAP * level_groups(fields, levels)[group][2]
        return pltpu.make_async_remote_copy(
            src_ref=outbound[group].at[owner],
            dst_ref=arrived[group].at[pl.ds(step * rows, rows), :],
            send_sem=out_sem.at[group * ncol + step],
            recv_sem=in_sem.at[group * ncol + step],
            device_id=(row, owner),
            device_id_type=MESH,
        )

    for group, (start, stop, padded) in enumerate(level_groups(fields, levels)):
        lax.fori_loop(start, stop, one_level, 0)
        base = start * fields * tile_rows
        sums = None
        for t in range(tiles):
            per_row = []
            for g in range(coarse_rows):
                value = None
                for r in range(3 * g, 3 * g + 3):
                    term = weighted[t, pl.ds(base + r, padded, stride=tile_rows), :]
                    value = term if value is None else value + term
                per_row.append(value)
            fine = t * LANES + lax.broadcasted_iota(jnp.int32, (LANES, LANES), 0)
            name = lax.broadcasted_iota(jnp.int32, (LANES, LANES), 1)
            pick = (fine // 3 == name).astype(jnp.float32).astype(jnp.bfloat16)
            term = split_dot(jnp.concatenate(per_row, 0), pick)
            sums = term if sums is None else sums + term
        size = coarse_rows * padded
        coarse[0:size, :] = sums
        tag_row = lax.broadcasted_iota(jnp.int32, (padded, LANES), 0) == (stop - start) * fields
        blocks = []
        for g in range(coarse_rows):
            tag = (slot_ref[g] + 1).astype(jnp.float32)
            blocks.append(jnp.where(tag_row, tag, coarse[g * padded : (g + 1) * padded, :]))
        for k in range(ncol * CAP):
            value = None
            for g in range(coarse_rows):
                term = jnp.where(spots[g] == k, 1.0, 0.0) * blocks[g]
                value = term if value is None else value + term
            outbound[group][k // CAP, (k % CAP) * padded : (k % CAP + 1) * padded, :] = value
        for step in range(1, ncol):
            to_owner(group, step).start()
        arrived[group][0 : CAP * padded, :] = outbound[group][col]

    groups = len(level_groups(fields, levels))
    for group in range(groups):
        for step in range(1, ncol):
            to_owner(group, step).wait_recv()

    for way in range(8):

        @pl.when(exists(way))
        def _(way=way):
            remote(way).wait_send()
            if way in (NORTH, SOUTH):
                for side in range(2):
                    own_columns(way, side, False).wait_send()

    for group in range(groups):
        for step in range(1, ncol):
            to_owner(group, step).wait_send()


def finish(dims, nest, *refs):
    fields, levels, tiles, ncol = dims
    groups = level_groups(fields, levels)
    arrived = refs[: len(groups)]
    nest_hbm, parent_ref, store_sem = refs[len(groups) :]
    stores = []
    for t in range(tiles):
        copy = pltpu.make_async_copy(
            nest.at[t], nest_hbm.at[:, t * LANES : (t + 1) * LANES], store_sem.at[t]
        )
        copy.start()
        stores.append(copy)

    count = ncol * CAP
    start, stop, padded = groups[0]
    tags = arrived[0][pl.ds((stop - start) * fields, count, stride=padded), :]
    parent_row = lax.broadcasted_iota(jnp.int32, (count, LANES), 1).astype(jnp.float32) + 1.0
    picked = (tags == parent_row).astype(jnp.float32)
    stack = jnp.concatenate(
        [picked, picked, jnp.zeros((LANES - 2 * count, LANES), jnp.float32)], 0
    )
    picker = stack.T[:PROWS].astype(jnp.bfloat16)
    filler = jnp.zeros((LANES - 2 * count, LANES), jnp.bfloat16)
    for ref, (start, stop, padded) in zip(arrived, groups):
        for level in range(start, stop):
            for f in range(fields):
                at = (level - start) * fields + f
                value = ref[pl.ds(at, count, stride=padded), :]
                high = value.astype(jnp.bfloat16)
                low = (value - high.astype(jnp.float32)).astype(jnp.bfloat16)
                parent_ref[f * levels + level] = jnp.dot(
                    picker,
                    jnp.concatenate([high, low, filler], 0),
                    preferred_element_type=jnp.float32,
                )
    for copy in stores:
        copy.wait()


def shards(adjoint_field, advect_x, advect_y, diffusion, zone_cells, feedback_dest, feedback_slot):
    fields, levels, tile_rows, tile_cols = adjoint_field.shape
    planes = fields * levels
    tiles = tile_cols // LANES
    nrow, ncol = lax.axis_size("row"), lax.axis_size("col")
    planes_pad = round_up(planes, SUB)
    levels_pad = round_up(levels, SUB)
    total = 2 * planes_pad + 2 * levels_pad
    own = (tiles, planes * tile_rows, LANES)
    level_own = (tiles, levels * tile_rows, LANES)
    f32 = jnp.float32
    vmem = pltpu.VMEM
    dma = pltpu.SemaphoreType.DMA
    smem_spec = pl.BlockSpec(memory_space=pltpu.SMEM)
    any_spec = pl.BlockSpec(memory_space=pl.ANY)
    nest_shape = (tiles, planes * tile_rows, LANES)
    groups = level_groups(fields, levels)
    reach = max(start * fields + padded for start, _, padded in groups)
    most = max(padded for _, _, padded in groups)
    vmem_spec = pl.BlockSpec(memory_space=pltpu.VMEM)
    nest, *arrived = pl.pallas_call(
        functools.partial(kernel, (fields, levels, tile_rows, tiles)),
        out_shape=[pltpu.VMEM(nest_shape, f32)]
        + [pltpu.VMEM((ncol * CAP * padded, LANES), f32) for _, _, padded in groups],
        in_specs=[smem_spec] * 3 + [any_spec] * 4,
        out_specs=[vmem_spec] * (1 + len(groups)),
        scratch_shapes=[vmem((ncol, CAP * padded, LANES), f32) for _, _, padded in groups]
        + [
            vmem(own, f32),
            vmem((tiles, planes * tile_rows, LANES), f32),
            vmem(level_own, f32),
            vmem(level_own, f32),
            vmem((tiles, total * SUB, LANES), f32),
            vmem((tiles, tile_rows, LANES), f32),
            vmem((tiles, tile_rows, LANES), f32),
            vmem((tile_rows // 3 * most, LANES), f32),
        ]
        + [vmem((ITERS * tiles, total, LANES), f32)] * 4
        + [vmem((3, tile_rows, LANES), f32)] * 4
        + [
            vmem((4, 3, SUB, LANES), f32),
            vmem((4, 3, SUB, LANES), f32),
            vmem((2, ITERS, tile_rows + SUB, LANES), f32),
            vmem((tiles, reach * tile_rows, LANES), f32),
            dma((4 * tiles,)),
            dma((12,)),
            dma((12,)),
            dma((len(groups) * ncol,)),
            dma((len(groups) * ncol,)),
        ],
        compiler_params=pltpu.CompilerParams(
            collective_id=0, has_side_effects=True, vmem_limit_bytes=61 * 1024 * 1024
        ),
    )(
        zone_cells,
        feedback_dest.reshape(-1),
        feedback_slot.reshape(-1),
        adjoint_field.reshape(planes * tile_rows, tile_cols),
        diffusion.reshape(planes * tile_rows, tile_cols),
        advect_x.reshape(levels * tile_rows, tile_cols),
        advect_y.reshape(levels * tile_rows, tile_cols),
    )
    nest, parent = pl.pallas_call(
        functools.partial(finish, (fields, levels, tiles, ncol)),
        out_shape=(
            jax.ShapeDtypeStruct((planes * tile_rows, tile_cols), f32),
            jax.ShapeDtypeStruct((planes, PROWS, LANES), f32),
        ),
        in_specs=[vmem_spec] * (1 + len(groups)),
        out_specs=(any_spec, vmem_spec),
        scratch_shapes=[dma((tiles,))],
        compiler_params=pltpu.CompilerParams(vmem_limit_bytes=16 * 1024 * 1024),
    )(nest, *arrived)
    return (
        nest.reshape(adjoint_field.shape),
        parent.reshape(fields, levels, PROWS, LANES),
    )


def solution(mesh):
    placed = (
        P(None, None, "row", "col"),
        P(None, "row", "col"),
        P(None, "row", "col"),
        P(None, None, "row", "col"),
        P(),
        P("col", "row", None),
        P("col", "row", None),
    )
    return jax.shard_map(
        shards,
        mesh=mesh,
        in_specs=placed,
        out_specs=(P(None, None, "row", "col"), P(None, None, "row", "col")),
        check_vma=False,
    )
```

```python
import functools

import jax
import jax.numpy as jnp
from jax import lax
from jax.experimental import pallas as pl
from jax.experimental.pallas import tpu as pltpu
from jax.sharding import PartitionSpec as P

ITERS = 3
PROWS = 80
CAP = 2
LANES = 128
SUB = 8
PACK = 4
MESH = pl.DeviceIdType.MESH
DIRS = ((-1, 0), (1, 0), (0, 1), (0, -1), (-1, 1), (-1, -1), (1, 1), (1, -1))
NORTH, SOUTH, EAST, WEST, NE, NW, SE, SW = range(8)
OPPOSITE = (SOUTH, NORTH, WEST, EAST, SW, SE, NW, NE)


def round_up(value, step):
    return -(-value // step) * step


def level_groups(fields, levels):
    groups, start = [], 0
    while start < levels:
        stop = start + -(-(levels - start) // 2)
        groups.append((start, stop, round_up((stop - start) * fields + 1, SUB)))
        start = stop
    return groups


def split_dot(values, weights):
    high = values.astype(jnp.bfloat16)
    low = (values - high.astype(jnp.float32)).astype(jnp.bfloat16)
    return jnp.dot(high, weights, preferred_element_type=jnp.float32) + jnp.dot(
        low, weights, preferred_element_type=jnp.float32
    )


def kernel(
    dims,
    zone_ref,
    dest_ref,
    slot_ref,
    field_hbm,
    spread_hbm,
    along_x_hbm,
    along_y_hbm,
    *refs,
):
    count_groups = len(level_groups(dims[0], dims[1]))
    nest, arrived = refs[0], refs[1 : 1 + count_groups]
    outbound = refs[1 + count_groups : 1 + 2 * count_groups]
    (
    field,
    spread,
    along_x,
    along_y,
    halo,
    keep,
    weigh,
    coarse,
    rows_n,
    rows_s,
    got_n,
    got_s,
    slab_e,
    slab_w,
    got_e,
    got_w,
    got_corner,
    got_own,
    edges,
    weighted,
    load_sem,
    send_sem,
    recv_sem,
    out_sem,
    in_sem,
    ) = refs[1 + 2 * count_groups :]
    fields, levels, tile_rows, tiles = dims
    planes = fields * levels
    spread_at = round_up(planes, SUB)
    x_at = 2 * spread_at
    y_at = x_at + round_up(levels, SUB)
    total = y_at + round_up(levels, SUB)
    planes_pad = spread_at
    row, col = lax.axis_index("row"), lax.axis_index("col")
    nrow, ncol = lax.axis_size("row"), lax.axis_size("col")
    wide = tile_rows + SUB

    def exists(way):
        down, over = DIRS[way]
        conditions = []
        if down < 0:
            conditions.append(row > 0)
        if down > 0:
            conditions.append(row < nrow - 1)
        if over < 0:
            conditions.append(col > 0)
        if over > 0:
            conditions.append(col < ncol - 1)
        return functools.reduce(jnp.logical_and, conditions)

    def device(way):
        return (row + DIRS[way][0], col + DIRS[way][1])

    barrier = pltpu.get_barrier_semaphore()
    for way in (NORTH, SOUTH, NE, NW, SE, SW):

        @pl.when(exists(way))
        def _(way=way):
            pl.semaphore_signal(barrier, inc=1, device_id=device(way), device_id_type=MESH)

    for step in range(1, ncol):
        pl.semaphore_signal(
            barrier, inc=1, device_id=(row, lax.rem(col + step, ncol)), device_id_type=MESH
        )

    loads = []
    for kind, (source, target) in enumerate(
        ((field_hbm, field), (spread_hbm, spread), (along_x_hbm, along_x), (along_y_hbm, along_y))
    ):
        count = source.shape[0]
        for t in range(tiles):
            copy = pltpu.make_async_copy(
                source.at[:, t * LANES : (t + 1) * LANES],
                target.at[t, 0:count, :],
                load_sem.at[kind * tiles + t],
            )
            copy.start()
            loads.append(copy)

    row_index = row * tile_rows + lax.broadcasted_iota(jnp.int32, (tile_rows, LANES), 0)
    lane = lax.broadcasted_iota(jnp.int32, (tile_rows, LANES), 1)
    grid_rows, grid_cols = tile_rows * nrow, tiles * LANES * ncol

    def ramp(position, count, low_zone, high_zone):
        scale_low = jnp.full((tile_rows, LANES), (low_zone + 1).astype(jnp.float32))
        scale_high = jnp.full((tile_rows, LANES), (high_zone + 1).astype(jnp.float32))
        lower = jnp.maximum(low_zone - position, 0).astype(jnp.float32) / scale_low
        upper = jnp.maximum(high_zone - (count - 1 - position), 0).astype(jnp.float32) / scale_high
        return jnp.maximum(lower, upper)

    weight_rows = ramp(row_index, grid_rows, zone_ref[0], zone_ref[1])
    for t in range(tiles):
        weight_cols = ramp((col * tiles + t) * LANES + lane, grid_cols, zone_ref[2], zone_ref[3])
        relaxation = jnp.maximum(weight_rows, weight_cols)
        keep[t] = 1.0 - relaxation
        weigh[t] = (1.0 - relaxation) / 9.0 + relaxation
    halo[...] = jnp.zeros_like(halo)
    received = {NORTH: got_n, SOUTH: got_s, EAST: got_e, WEST: got_w}
    for place, way in enumerate((NE, NW, SE, SW)):
        received[way] = got_corner.at[place]
    for way in range(8):

        @pl.when(jnp.logical_not(exists(way)))
        def _(way=way):
            received[way][...] = jnp.zeros(received[way].shape, jnp.float32)
            if way in (NORTH, SOUTH):
                for side in range(2):
                    shape = got_own.shape[1:]
                    got_own[2 * side + way] = jnp.zeros(shape, jnp.float32)

    for copy in loads:
        copy.wait()

    for kind, pieces in enumerate(
        (((field, planes, 0),), ((spread, planes, 0),), ((along_x, levels, 0), (along_y, levels, 8)))
    ):
        first = jnp.zeros((tile_rows, LANES), jnp.float32)
        last = jnp.zeros((tile_rows, LANES), jnp.float32)
        for source, count, base in pieces:

            def pack(p, carry, source=source, base=base):
                first, last = carry
                at = pl.multiple_of(p * tile_rows, SUB)
                here = lane // PACK == p + base
                moved_first = pltpu.roll(source[0, pl.ds(at, tile_rows), :], PACK * (p + base), 1)
                moved_last = pltpu.roll(
                    source[tiles - 1, pl.ds(at, tile_rows), :], PACK * (p + base + 1), 1
                )
                return jnp.where(here, moved_first, first), jnp.where(here, moved_last, last)

            first, last = lax.fori_loop(0, count, pack, (first, last), unroll=6)
        slab_w[kind] = first
        slab_e[kind] = last

    top, bottom = slice(0, SUB), slice(tile_rows - SUB, tile_rows)
    sources = {
        NORTH: rows_n,
        SOUTH: rows_s,
        EAST: slab_e,
        WEST: slab_w,
        NE: slab_e.at[:, top, :],
        NW: slab_w.at[:, top, :],
        SE: slab_e.at[:, bottom, :],
        SW: slab_w.at[:, bottom, :],
    }

    def remote(way):
        back = OPPOSITE[way]
        return pltpu.make_async_remote_copy(
            src_ref=sources[way],
            dst_ref=received[back],
            send_sem=send_sem.at[way],
            recv_sem=recv_sem.at[back],
            device_id=device(way),
            device_id_type=MESH,
        )

    def own_columns(way, side, arriving):
        back = OPPOSITE[way]
        sent = back if arriving else way
        place = 2 * side + (way if arriving else back)
        slab = (slab_e, slab_w)[side]
        return pltpu.make_async_remote_copy(
            src_ref=slab.at[:, top if sent == NORTH else bottom, :],
            dst_ref=got_own.at[place],
            send_sem=send_sem.at[8 + 2 * side + sent],
            recv_sem=recv_sem.at[8 + place],
            device_id=device(way),
            device_id_type=MESH,
        )

    greeted = jnp.int32(ncol - 1)
    for way in (NORTH, SOUTH, NE, NW, SE, SW):
        greeted = greeted + exists(way).astype(jnp.int32)
    pl.semaphore_wait(barrier, greeted)

    for way in range(8):

        @pl.when(exists(way))
        def _(way=way):
            if way in (NORTH, SOUTH):
                for side in range(2):
                    own_columns(way, side, False).start()
            else:
                remote(way).start()

    for r in range(ITERS):
        for t in range(tiles):
            for source, count, base in (
                (field, planes, 0),
                (spread, planes, spread_at),
                (along_x, levels, x_at),
                (along_y, levels, y_at),
            ):
                rows_n[r * tiles + t, base : base + count, :] = source[
                    t, pl.ds(r, count, stride=tile_rows), :
                ]
                rows_s[r * tiles + t, base : base + count, :] = source[
                    t, pl.ds(tile_rows - ITERS + r, count, stride=tile_rows), :
                ]

    for way in (NORTH, SOUTH):

        @pl.when(exists(way))
        def _(way=way):
            remote(way).start()

    for way in range(8):

        @pl.when(exists(way))
        def _(way=way):
            pltpu.make_async_remote_copy(
                src_ref=sources[OPPOSITE[way]],
                dst_ref=received[way],
                send_sem=send_sem.at[OPPOSITE[way]],
                recv_sem=recv_sem.at[way],
                device_id=device(way),
                device_id_type=MESH,
            ).wait_recv()
            if way in (NORTH, SOUTH):
                for side in range(2):
                    own_columns(way, side, True).wait_recv()

    for r in range(ITERS):
        for t in range(tiles):
            halo[t, pl.ds(r, total, stride=SUB), :] = got_s[r * tiles + t]
            halo[t, pl.ds(SUB - ITERS + r, total, stride=SUB), :] = got_n[r * tiles + t]

    lane_wide = lax.broadcasted_iota(jnp.int32, (wide, LANES), 1)
    lane_low = lax.broadcasted_iota(jnp.int32, (SUB, LANES), 1)
    south_half = lax.broadcasted_iota(jnp.int32, (SUB, LANES), 0) < SUB // 2

    def block(source, p, base):
        at = pl.multiple_of(p * tile_rows, SUB)
        low = pl.multiple_of((p + base) * SUB, SUB)
        return [
            jnp.concatenate([source[t, pl.ds(at, tile_rows), :], halo[t, pl.ds(low, SUB), :]], 0)
            for t in range(tiles)
        ]

    def advance(now, d, half_x, half_y, rights, lefts, count):
        later = []
        for t in range(count):
            value = now[t] * (1.0 - 4.0 * d[t])
            value = value + pltpu.roll(now[t] * (d[t] + half_x[t]), wide - 1, 0)
            value = value + pltpu.roll(now[t] * (d[t] - half_x[t]), 1, 0)
            later.append(value + rights[t] + lefts[t])
        return later

    def with_rows(slab, kind, from_south, from_north):
        return jnp.concatenate([slab[kind], jnp.where(south_half, from_south, from_north)], 0)

    period = PACK * levels

    def each_field(slab, base):
        value = None
        for f in range(fields):
            moved = pltpu.roll(slab, (period * f - PACK * base) % LANES, 1)
            value = moved if value is None else jnp.where(lane_wide >= period * f, moved, value)
        return value

    inner = lane_wide % PACK
    for side in range(2):
        own, other = ((slab_e, got_e), (slab_w, got_w))[side]
        below, above = ((2, 0), (3, 1))[side]
        kinds = []
        for kind in range(3):
            pair = [
                with_rows(own, kind, got_own[2 * side + SOUTH, kind], got_own[2 * side + NORTH, kind]),
                with_rows(other, kind, got_corner[below, kind], got_corner[above, kind]),
            ]
            kinds.append(pair if side == 0 else pair[::-1])
        now, d, along = kinds
        half_x = [0.5 * each_field(part, 0) for part in along]
        half_y = [0.5 * each_field(part, 8) for part in along]
        for sweep in range(ITERS):
            right = [now[t] * (d[t] + half_y[t]) for t in range(2)]
            left = [now[t] * (d[t] - half_y[t]) for t in range(2)]
            edges[side, sweep] = right[1] if side == 0 else left[0]
            if sweep < ITERS - 1:
                rights = [
                    jnp.where(
                        inner == PACK - 1,
                        pltpu.roll(right[1], PACK - 1, 1),
                        pltpu.roll(right[0], LANES - 1, 1),
                    ),
                    pltpu.roll(right[1], LANES - 1, 1),
                ]
                lefts = [
                    pltpu.roll(left[0], 1, 1),
                    jnp.where(
                        inner == 0,
                        pltpu.roll(left[0], LANES - PACK + 1, 1),
                        pltpu.roll(left[1], 1, 1),
                    ),
                ]
                now = advance(now, d, half_x, half_y, rights, lefts, 2)

    def one_level(level, _):
        half_x = [0.5 * part for part in block(along_x, level, x_at)]
        half_y = [0.5 * part for part in block(along_y, level, y_at)]

        def one_field(f, _):
            p = f * levels + level
            now = block(field, p, 0)
            d = block(spread, p, spread_at)
            for sweep in range(ITERS):
                right = [
                    pltpu.roll(now[t] * (d[t] + half_y[t]), LANES - 1, 1) for t in range(tiles)
                ]
                left = [pltpu.roll(now[t] * (d[t] - half_y[t]), 1, 1) for t in range(tiles)]
                right.append(pltpu.roll(edges[0, sweep], LANES - 1 - PACK * p, 1))
                left.append(pltpu.roll(edges[1, sweep], LANES - PACK + 1 - PACK * p, 1))
                rights = [
                    jnp.where(lane_wide == LANES - 1, right[t + 1], right[t]) for t in range(tiles)
                ]
                lefts = [jnp.where(lane_wide == 0, left[t - 1], left[t]) for t in range(tiles)]
                now = advance(now, d, half_x, half_y, rights, lefts, tiles)
            at = pl.multiple_of(p * tile_rows, SUB)
            to = pl.multiple_of((level * fields + f) * tile_rows, SUB)
            for t in range(tiles):
                final = now[t][:tile_rows]
                nest[t, pl.ds(at, tile_rows), :] = keep[t] * final
                weighted[t, pl.ds(to, tile_rows), :] = weigh[t] * final
            return 0

        return lax.fori_loop(0, fields, one_field, 0)

    coarse_rows = tile_rows // 3
    dests = [dest_ref[g] for g in range(coarse_rows)]
    spots = []
    for g in range(coarse_rows):
        rank = jnp.int32(0)
        for before in range(g):
            rank = rank + jnp.where(dests[before] == dests[g], 1, 0)
        spots.append(dests[g] * CAP + rank)

    def to_owner(group, step):
        owner = lax.rem(col + step, ncol)
        rows = CAP * level_groups(fields, levels)[group][2]
        return pltpu.make_async_remote_copy(
            src_ref=outbound[group].at[owner],
            dst_ref=arrived[group].at[pl.ds(step * rows, rows), :],
            send_sem=out_sem.at[group * ncol + step],
            recv_sem=in_sem.at[group * ncol + step],
            device_id=(row, owner),
            device_id_type=MESH,
        )

    for group, (start, stop, padded) in enumerate(level_groups(fields, levels)):
        lax.fori_loop(start, stop, one_level, 0)
        base = start * fields * tile_rows
        sums = None
        for t in range(tiles):
            per_row = []
            for g in range(coarse_rows):
                value = None
                for r in range(3 * g, 3 * g + 3):
                    term = weighted[t, pl.ds(base + r, padded, stride=tile_rows), :]
                    value = term if value is None else value + term
                per_row.append(value)
            fine = t * LANES + lax.broadcasted_iota(jnp.int32, (LANES, LANES), 0)
            name = lax.broadcasted_iota(jnp.int32, (LANES, LANES), 1)
            pick = (fine // 3 == name).astype(jnp.float32).astype(jnp.bfloat16)
            term = split_dot(jnp.concatenate(per_row, 0), pick)
            sums = term if sums is None else sums + term
        size = coarse_rows * padded
        coarse[0:size, :] = sums
        tag_row = lax.broadcasted_iota(jnp.int32, (padded, LANES), 0) == (stop - start) * fields
        blocks = []
        for g in range(coarse_rows):
            tag = (slot_ref[g] + 1).astype(jnp.float32)
            blocks.append(jnp.where(tag_row, tag, coarse[g * padded : (g + 1) * padded, :]))
        for k in range(ncol * CAP):
            value = None
            for g in range(coarse_rows):
                term = jnp.where(spots[g] == k, 1.0, 0.0) * blocks[g]
                value = term if value is None else value + term
            outbound[group][k // CAP, (k % CAP) * padded : (k % CAP + 1) * padded, :] = value
        for step in range(1, ncol):
            to_owner(group, step).start()
        arrived[group][0 : CAP * padded, :] = outbound[group][col]

    groups = len(level_groups(fields, levels))
    for group in range(groups):
        for step in range(1, ncol):
            to_owner(group, step).wait_recv()

    for way in range(8):

        @pl.when(exists(way))
        def _(way=way):
            remote(way).wait_send()
            if way in (NORTH, SOUTH):
                for side in range(2):
                    own_columns(way, side, False).wait_send()

    for group in range(groups):
        for step in range(1, ncol):
            to_owner(group, step).wait_send()


def finish(dims, nest, *refs):
    fields, levels, tiles, ncol = dims
    groups = level_groups(fields, levels)
    arrived = refs[: len(groups)]
    nest_hbm, parent_ref, store_sem = refs[len(groups) :]
    stores = []
    for t in range(tiles):
        copy = pltpu.make_async_copy(
            nest.at[t], nest_hbm.at[:, t * LANES : (t + 1) * LANES], store_sem.at[t]
        )
        copy.start()
        stores.append(copy)

    count = ncol * CAP
    start, stop, padded = groups[0]
    tags = arrived[0][pl.ds((stop - start) * fields, count, stride=padded), :]
    parent_row = lax.broadcasted_iota(jnp.int32, (count, LANES), 1).astype(jnp.float32) + 1.0
    picked = (tags == parent_row).astype(jnp.float32)
    stack = jnp.concatenate(
        [picked, picked, jnp.zeros((LANES - 2 * count, LANES), jnp.float32)], 0
    )
    picker = stack.T[:PROWS].astype(jnp.bfloat16)
    filler = jnp.zeros((LANES - 2 * count, LANES), jnp.bfloat16)
    for ref, (start, stop, padded) in zip(arrived, groups):
        for level in range(start, stop):
            for f in range(fields):
                at = (level - start) * fields + f
                value = ref[pl.ds(at, count, stride=padded), :]
                high = value.astype(jnp.bfloat16)
                low = (value - high.astype(jnp.float32)).astype(jnp.bfloat16)
                parent_ref[f * levels + level] = jnp.dot(
                    picker,
                    jnp.concatenate([high, low, filler], 0),
                    preferred_element_type=jnp.float32,
                )
    for copy in stores:
        copy.wait()


def shards(adjoint_field, advect_x, advect_y, diffusion, zone_cells, feedback_dest, feedback_slot):
    fields, levels, tile_rows, tile_cols = adjoint_field.shape
    planes = fields * levels
    tiles = tile_cols // LANES
    nrow, ncol = lax.axis_size("row"), lax.axis_size("col")
    planes_pad = round_up(planes, SUB)
    levels_pad = round_up(levels, SUB)
    total = 2 * planes_pad + 2 * levels_pad
    own = (tiles, planes * tile_rows, LANES)
    level_own = (tiles, levels * tile_rows, LANES)
    f32 = jnp.float32
    vmem = pltpu.VMEM
    dma = pltpu.SemaphoreType.DMA
    smem_spec = pl.BlockSpec(memory_space=pltpu.SMEM)
    any_spec = pl.BlockSpec(memory_space=pl.ANY)
    nest_shape = (tiles, planes * tile_rows, LANES)
    groups = level_groups(fields, levels)
    reach = max(start * fields + padded for start, _, padded in groups)
    most = max(padded for _, _, padded in groups)
    vmem_spec = pl.BlockSpec(memory_space=pltpu.VMEM)
    nest, *arrived = pl.pallas_call(
        functools.partial(kernel, (fields, levels, tile_rows, tiles)),
        out_shape=[pltpu.VMEM(nest_shape, f32)]
        + [pltpu.VMEM((ncol * CAP * padded, LANES), f32) for _, _, padded in groups],
        in_specs=[smem_spec] * 3 + [any_spec] * 4,
        out_specs=[vmem_spec] * (1 + len(groups)),
        scratch_shapes=[vmem((ncol, CAP * padded, LANES), f32) for _, _, padded in groups]
        + [
            vmem(own, f32),
            vmem((tiles, planes * tile_rows, LANES), f32),
            vmem(level_own, f32),
            vmem(level_own, f32),
            vmem((tiles, total * SUB, LANES), f32),
            vmem((tiles, tile_rows, LANES), f32),
            vmem((tiles, tile_rows, LANES), f32),
            vmem((tile_rows // 3 * most, LANES), f32),
        ]
        + [vmem((ITERS * tiles, total, LANES), f32)] * 4
        + [vmem((3, tile_rows, LANES), f32)] * 4
        + [
            vmem((4, 3, SUB, LANES), f32),
            vmem((4, 3, SUB, LANES), f32),
            vmem((2, ITERS, tile_rows + SUB, LANES), f32),
            vmem((tiles, reach * tile_rows, LANES), f32),
            dma((4 * tiles,)),
            dma((12,)),
            dma((12,)),
            dma((len(groups) * ncol,)),
            dma((len(groups) * ncol,)),
        ],
        compiler_params=pltpu.CompilerParams(
            collective_id=0, has_side_effects=True, vmem_limit_bytes=61 * 1024 * 1024
        ),
    )(
        zone_cells,
        feedback_dest.reshape(-1),
        feedback_slot.reshape(-1),
        adjoint_field.reshape(planes * tile_rows, tile_cols),
        diffusion.reshape(planes * tile_rows, tile_cols),
        advect_x.reshape(levels * tile_rows, tile_cols),
        advect_y.reshape(levels * tile_rows, tile_cols),
    )
    nest, parent = pl.pallas_call(
        functools.partial(finish, (fields, levels, tiles, ncol)),
        out_shape=(
            jax.ShapeDtypeStruct((planes * tile_rows, tile_cols), f32),
            jax.ShapeDtypeStruct((planes, PROWS, LANES), f32),
        ),
        in_specs=[vmem_spec] * (1 + len(groups)),
        out_specs=(any_spec, vmem_spec),
        scratch_shapes=[dma((tiles,))],
        compiler_params=pltpu.CompilerParams(vmem_limit_bytes=16 * 1024 * 1024),
    )(nest, *arrived)
    return (
        nest.reshape(adjoint_field.shape),
        parent.reshape(fields, levels, PROWS, LANES),
    )


def solution(mesh):
    placed = (
        P(None, None, "row", "col"),
        P(None, "row", "col"),
        P(None, "row", "col"),
        P(None, None, "row", "col"),
        P(),
        P("col", "row", None),
        P("col", "row", None),
    )
    return jax.shard_map(
        shards,
        mesh=mesh,
        in_specs=placed,
        out_specs=(P(None, None, "row", "col"), P(None, None, "row", "col")),
        check_vma=False,
    )
```
